32 devices in a mesh: dom: 8 (over y, x, core), rep: 4 (over z).
Axes of the slice: x: 2, y: 2, z: 4, core: 2. Of those that a mesh axis runs over, the one named last changes fastest.
Arguments:
- hop_feats: bfloat16 [3, 65536, 128], P(None, ('dom', 'rep')), may hold values from -6 to 6
- adj_local: bfloat16 [512, 12, 128, 128], P(('dom', 'rep')), may hold values from -0.125 to 0.125
- local_cols: int32 [512, 12], P(('dom', 'rep')), may hold values from 0 to 15
- adj_halo: bfloat16 [512, 4, 128, 128], P(('dom', 'rep')), may hold values from -0.125 to 0.125
- halo_cols: int32 [512, 4], P(('dom', 'rep')), may hold values from 0 to 3
- boundary_rows: int32 [32, 512], P(('dom', 'rep')), may hold values from 0 to 2047
- train_ids: int32 [32, 2048], P(('dom', 'rep')), may hold values from 0 to 2047, as said below
- shuffle: int32 [32, 2048], P(('dom', 'rep')), may hold values from 0 to 2047, as said below
- labels: int32 [65536], P(('dom', 'rep')), may hold values from 0 to 171
- labelled: int32 [65536], P(('dom', 'rep')), may hold values from 0 to 1
- w_first: bfloat16 [512, 1024], P(None, 'rep'), may hold values from -1 to 1
- w_second: bfloat16 [1024, 172], P('rep'), may hold values from -2 to 2
Outputs:
- next_hop: bfloat16 [65536, 128], P(('dom', 'rep'))
- batch_loss: float32 [32, 32], P(('dom', 'rep'))
- grad_first: float32 [512, 1024], P('dom', 'rep')
- grad_second: float32 [1024, 172], P('rep')
The draws below stay inside these ranges and needn't reach their ends.
Inputs may be any that keep to these rules, and one draw needn't show every extreme that they name: `local_cols`: local tile indices of the partition's own row tiles. `halo_cols`: indices of received boundary tiles. `boundary_rows`: rows of the sending partition itself. `train_ids`: rows of the partition itself. `shuffle`: each row is a permutation of 0 .. 2047.
All inputs are finite; a program needn't handle non-finite values.
Results may differ from the reference program's by a relative error of at most 0.005.
The reference program's roundings to bfloat16 on the way count: a program that leaves them out, or rounds other values in their place, can miss the bound.
Values may be sent and summed in bfloat16 or wider, within the bound.
No kernel may reach another device: no remote copies, remote signals or barrier semaphores. Data moves between devices by JAX's collectives and lax.ppermute only.
A program may use at most 128 MiB of HBM per device.

```python
import math
import jax
import jax.numpy as jnp
from jax import lax

D_FEAT = 128
HIDDEN_UNITS = 1024
CLASSES = 172
TILE = 128
RT = 16
KL = 12
KH = 4
HALO_TILES = 4
SLOTS = 2048
NODES = 65536
N_DOM = 8
N_REP = 4
DEVICES = 32


def slot_parts(key):
    train_ids = jax.random.randint(jax.random.fold_in(key, 11), (DEVICES, SLOTS), 0, RT * TILE)
    row_keys = jax.random.split(jax.random.fold_in(key, 12), DEVICES)
    shuffle = jax.vmap(lambda one_key: jax.random.permutation(one_key, SLOTS))(row_keys).astype(jnp.int32)
    return (train_ids.astype(jnp.int32), shuffle)


def draw_hop_feats(key, part):
    base = jnp.clip(jax.random.normal(jax.random.fold_in(key, 1), (3, NODES, D_FEAT), jnp.float32), -6.0, 6.0)
    return base.astype(jnp.bfloat16)


def draw_w_first(key, part):
    width = 4 * D_FEAT
    scale = 1.0 / math.sqrt(width)
    base = jnp.clip(jax.random.normal(jax.random.fold_in(key, 4), (width, HIDDEN_UNITS), jnp.float32), -6.0, 6.0) * scale
    return base.astype(jnp.bfloat16)


def draw_w_second(key, part):
    scale = 1.0 / math.sqrt(HIDDEN_UNITS)
    base = jnp.clip(jax.random.normal(jax.random.fold_in(key, 5), (HIDDEN_UNITS, CLASSES), jnp.float32), -6.0, 6.0) * scale
    return base.astype(jnp.bfloat16)


def draw_train_ids(key, part):
    return slot_parts(key)[0]


def draw_shuffle(key, part):
    return slot_parts(key)[1]


def draw_labelled(key, part):
    train_ids, shuffle = slot_parts(key)
    base = (jax.random.randint(jax.random.fold_in(key, 13), (NODES,), 0, 3) < 2).astype(jnp.int32)
    bases = jnp.arange(DEVICES, dtype=jnp.int32)[:, None] * (RT * TILE)
    order = bases + jnp.take_along_axis(train_ids, shuffle, axis=1)
    per = SLOTS // DEVICES
    batches = jnp.transpose(order.reshape(DEVICES, DEVICES, per), (1, 0, 2)).reshape(DEVICES, SLOTS)
    empty = jax.random.randint(jax.random.fold_in(key, 14), (2,), 0, DEVICES)
    cleared = batches[empty].reshape(-1)
    return base.at[cleared].set(0)


def touch_ends(entries, rng, least, largest):
    extent = entries.shape
    index_at = [jax.random.randint(jax.random.fold_in(rng, axis), (), 0, extent[axis]) for axis in range(len(extent))]
    entries = entries.at[tuple(index_at)].set(least)
    longest = extent.index(max(extent))
    index_at[longest] = (index_at[longest] + 1) % extent[longest]
    return entries.at[tuple(index_at)].set(largest)


def steps_of(rng, dims, pieces, least, largest):
    def one(axis_at, parts):
        draws = jax.random.uniform(jax.random.fold_in(jax.random.fold_in(rng, 6), axis_at), (parts,), jnp.float32, least / len(pieces), largest / len(pieces))
        return jnp.repeat(jnp.exp(draws), dims[axis_at] // parts).reshape((-1,) + (1,) * (len(dims) - axis_at - 1))

    gain = one(*pieces[0])
    for cut in pieces[1:]:
        gain = gain * one(*cut)
    return gain


def normal_values(key, extent, scale, most, shards=(), held_as=jnp.bfloat16):
    values = scale * jax.random.normal(key, extent, jnp.float32)
    if shards:
        values = values * steps_of(key, extent, shards, -0.22, 0.18)
    return jnp.clip(values, -most, most).astype(held_as)


def setup_inputs(seed: int = 0) -> dict:
    key_list = jax.random.split(jax.random.key(seed), 13)
    return {
        "hop_feats": draw_hop_feats(jax.random.fold_in(key_list[12], 71), 0),
        "adj_local": normal_values(key_list[1], (NODES // TILE, KL, TILE, TILE), (TILE * (KL + KH)) ** -0.5, 0.125, ((0, 32),)),
        "local_cols": touch_ends(jax.random.randint(key_list[2], (NODES // TILE, KL), 0, RT), jax.random.fold_in(key_list[2], 1), 0, RT - 1).astype(jnp.int32),
        "adj_halo": normal_values(key_list[3], (NODES // TILE, KH, TILE, TILE), (TILE * (KL + KH)) ** -0.5, 0.125, ((0, 32),)),
        "halo_cols": touch_ends(jax.random.randint(key_list[4], (NODES // TILE, KH), 0, HALO_TILES), jax.random.fold_in(key_list[4], 1), 0, HALO_TILES - 1).astype(jnp.int32),
        "boundary_rows": touch_ends(jax.random.randint(key_list[5], (DEVICES, HALO_TILES * TILE), 0, RT * TILE), jax.random.fold_in(key_list[5], 1), 0, (RT * TILE) - 1).astype(jnp.int32),
        "train_ids": draw_train_ids(jax.random.fold_in(key_list[12], 71), 0),
        "shuffle": draw_shuffle(jax.random.fold_in(key_list[12], 71), 0),
        "labels": touch_ends(jax.random.randint(key_list[8], (NODES,), 0, CLASSES), jax.random.fold_in(key_list[8], 1), 0, CLASSES - 1).astype(jnp.int32),
        "labelled": draw_labelled(jax.random.fold_in(key_list[12], 71), 0),
        "w_first": draw_w_first(jax.random.fold_in(key_list[12], 71), 0),
        "w_second": draw_w_second(jax.random.fold_in(key_list[12], 71), 0),
    }


def loss_head(logits, targets, weights_row):
    row_max = lax.optimization_barrier(jnp.max(logits, axis=1, keepdims=True))
    expos = jnp.exp(logits - row_max)
    totals = lax.optimization_barrier(jnp.sum(expos, axis=1, keepdims=True))
    classes = lax.broadcasted_iota(jnp.int32, logits.shape, 1)
    onehot = (classes == targets[:, None]).astype(jnp.float32)
    cross = jnp.log(totals[:, 0]) + row_max[:, 0] - lax.optimization_barrier(jnp.sum(onehot * logits, axis=1))
    count = jnp.maximum(jnp.sum(weights_row), 1.0)
    dlogits = ((expos / totals - onehot) * (weights_row / count)[:, None]).astype(jnp.bfloat16)
    return (cross, dlogits)

def source_losses(cross, weights_row, groups):
    masks = weights_row.reshape(groups, -1)
    sums = lax.optimization_barrier(jnp.sum(masks * cross.reshape(groups, -1), axis=1))
    return sums / jnp.maximum(lax.optimization_barrier(jnp.sum(masks, axis=1)), 1.0)

def batch_norm(pre):
    center = pre - lax.optimization_barrier(jnp.mean(pre, axis=-2, keepdims=True))
    rstd = lax.rsqrt(lax.optimization_barrier(jnp.mean(center * center, axis=-2, keepdims=True)) + 1e-05)
    return (center * rstd, rstd)

def norm_back(grad, normed, rstd):
    mean_grad = lax.optimization_barrier(jnp.mean(grad, axis=-2, keepdims=True))
    mean_proj = lax.optimization_barrier(jnp.mean(grad * normed, axis=-2, keepdims=True))
    return (grad - mean_grad - normed * mean_proj) * rstd

def reference(hop_feats, adj_local, local_cols, adj_halo, halo_cols, boundary_rows, train_ids, shuffle, labels, labelled, w_first, w_second):
    devices = N_DOM * N_REP
    rows = RT * TILE
    share = HALO_TILES * TILE // devices
    hop_two = hop_feats[2]
    bases = jnp.arange(devices, dtype=jnp.int32)[:, None] * rows
    sources = (bases + boundary_rows).reshape(devices, devices, share)
    halo_ids = jnp.transpose(sources, (1, 0, 2)).reshape(devices, devices * share)
    loc_tiles = adj_local.reshape(devices, RT, KL, TILE, TILE)
    loc_cols = local_cols.reshape(devices, RT, KL)
    far_tiles = adj_halo.reshape(devices, RT, KH, TILE, TILE)
    far_cols = halo_cols.reshape(devices, RT, KH)

    def one_part(part):
        own = lax.dynamic_slice_in_dim(hop_two, part * rows, rows, 0)
        own = own.reshape(RT, TILE, D_FEAT).astype(jnp.float32)
        halo = hop_two[halo_ids[part]].reshape(HALO_TILES, TILE, D_FEAT).astype(jnp.float32)
        summed = jnp.einsum('ikab,ikbc->iac', loc_tiles[part].astype(jnp.float32), own[loc_cols[part]])
        summed = summed + jnp.einsum('ikab,ikbc->iac', far_tiles[part].astype(jnp.float32), halo[far_cols[part]])
        return summed.reshape(rows, D_FEAT).astype(jnp.bfloat16)
    next_hop = lax.map(one_part, jnp.arange(devices, dtype=jnp.int32)).reshape(devices * rows, D_FEAT)
    order = bases + jnp.take_along_axis(train_ids, shuffle, axis=1)
    per = SLOTS // devices
    batches = jnp.transpose(order.reshape(devices, devices, per), (1, 0, 2)).reshape(devices, SLOTS)
    allfeat = jnp.concatenate([hop_feats[0], hop_feats[1], hop_feats[2], next_hop], axis=1)

    def one_batch(carry, node_ids):
        grad_one, grad_two = carry
        inputs = allfeat[node_ids]
        targets = labels[node_ids]
        weights_row = labelled[node_ids].astype(jnp.float32)
        hidden_pre = jnp.dot(inputs, w_first, preferred_element_type=jnp.float32)
        normed, rstd = batch_norm(hidden_pre)
        hidden = jnp.maximum(normed, 0.0).astype(jnp.bfloat16)
        logits = jnp.dot(hidden, w_second, preferred_element_type=jnp.float32)
        cross, dlogits = loss_head(logits, targets, weights_row)
        loss = source_losses(cross, weights_row, devices)
        grad_two = grad_two + jnp.dot(hidden.T, dlogits, preferred_element_type=jnp.float32)
        dhidden = jnp.dot(dlogits, w_second.T, preferred_element_type=jnp.float32)
        masked = jnp.where(normed > 0, dhidden, 0.0)
        dpre = norm_back(masked, normed, rstd).astype(jnp.bfloat16)
        grad_one = grad_one + jnp.dot(inputs.T, dpre, preferred_element_type=jnp.float32)
        return ((grad_one, grad_two), loss)
    start = (jnp.zeros((4 * D_FEAT, HIDDEN_UNITS), jnp.float32), jnp.zeros((HIDDEN_UNITS, CLASSES), jnp.float32))
    (grad_first, grad_second), batch_loss = lax.scan(one_batch, start, batches)
    return (next_hop, batch_loss, grad_first, grad_second)
```

```python
import math

import jax
import jax.numpy as jnp
from jax import lax
from jax.experimental import pallas as pl
from jax.experimental.pallas import tpu as pltpu
from jax.sharding import PartitionSpec as P

BOTH = ("dom", "rep")


def tile_sum_kernel(cols, tiles, table, *rest):
    base, out = (rest[0], rest[1]) if len(rest) == 2 else (None, rest[0])
    step = pl.program_id(0)
    block, depth = tiles.shape[0], tiles.shape[1]
    size = tiles.shape[2]
    for i in range(block):
        left = jnp.concatenate([tiles[i, k] for k in range(depth)], axis=1)
        right = jnp.concatenate(
            [table[cols[(step * block + i) * depth + k]] for k in range(depth)], axis=0
        )
        total = jnp.dot(left, right, preferred_element_type=jnp.float32)
        if base is not None:
            total = total + base[pl.ds(i * size, size), :]
        out[pl.ds(i * size, size), :] = total.astype(out.dtype)


def tile_sum(tiles, cols, table, base, dtype):
    count, depth, size, _ = tiles.shape
    width = table.shape[-1]
    block = math.gcd(count, max(1, 48 // depth))
    specs = [
        pl.BlockSpec((block, depth, size, size), lambda s, c: (s, 0, 0, 0)),
        pl.BlockSpec(table.shape, lambda s, c: (0, 0, 0)),
    ]
    operands = [tiles, table]
    if base is not None:
        specs.append(pl.BlockSpec((block * size, width), lambda s, c: (s, 0)))
        operands.append(base)
    return pl.pallas_call(
        tile_sum_kernel,
        grid_spec=pltpu.PrefetchScalarGridSpec(
            num_scalar_prefetch=1,
            grid=(count // block,),
            in_specs=specs,
            out_specs=pl.BlockSpec((block * size, width), lambda s, c: (s, 0)),
        ),
        out_shape=jax.ShapeDtypeStruct((count * size, width), dtype),
        name="tile_sum",
    )(cols.reshape(-1), *operands)


def pick_rows_kernel(order, hops, last, out):
    rows = hops.shape[1]
    ids = order[...]
    nodes = lax.broadcasted_iota(jnp.int32, (ids.shape[0], rows), 1)
    picks = jnp.where(ids == nodes, 1.0, 0.0).astype(jnp.bfloat16)
    table = jnp.concatenate([hops[0], hops[1], hops[2], last[...]], axis=1)
    out[...] = jnp.dot(picks, table, preferred_element_type=jnp.float32).astype(out.dtype)


def pick_rows(order, hops, last):
    slots = order.shape[0]
    width = hops.shape[2]
    block = 256
    return pl.pallas_call(
        pick_rows_kernel,
        grid=(slots // block,),
        in_specs=[
            pl.BlockSpec((block, 1), lambda s: (s, 0)),
            pl.BlockSpec(hops.shape, lambda s: (0, 0, 0)),
            pl.BlockSpec(last.shape, lambda s: (0, 0)),
        ],
        out_specs=pl.BlockSpec((block, 4 * width), lambda s: (s, 0)),
        out_shape=jax.ShapeDtypeStruct((slots, 4 * width), hops.dtype),
        name="pick_rows",
    )(order[:, None], hops, last)


def take_ints(tables, index, lanes):
    groups = tables[0].shape[0] // lanes
    parts = []
    for table in tables:
        grid = table.reshape(groups, lanes)
        parts += [grid // 128, grid % 128]
    stacked = jnp.concatenate(parts, axis=0).astype(jnp.bfloat16)
    low, high = index % lanes, index // lanes
    onehot = (lax.broadcasted_iota(jnp.int32, (lanes, index.shape[0]), 0) == low[None, :]).astype(jnp.bfloat16)
    found = jnp.dot(stacked, onehot, preferred_element_type=jnp.float32)
    found = found.reshape(len(tables), 2, groups, index.shape[0])
    mask = lax.broadcasted_iota(jnp.int32, (groups, index.shape[0]), 0) == high[None, :]
    sums = jnp.sum(jnp.where(mask[None, None], found, 0.0), axis=2).astype(jnp.int32)
    return [sums[t, 0] * 128 + sums[t, 1] for t in range(len(tables))]


def gather_by_exchange(value, axes, count):
    copies = jnp.broadcast_to(value, (count,) + value.shape[1:])
    return lax.all_to_all(copies, axes, split_axis=0, concat_axis=0, tiled=True)


def contract_rows(left, right):
    return lax.dot_general(
        left, right, (((0,), (0,)), ((), ())), preferred_element_type=jnp.float32
    )


def shards(
    hop_feats,
    adj_local,
    local_cols,
    adj_halo,
    halo_cols,
    boundary_rows,
    train_ids,
    shuffle,
    labels,
    labelled,
    w_first,
    w_second,
):
    num_dom = lax.axis_size("dom")
    num_rep = lax.axis_size("rep")
    devices = num_dom * num_rep
    tile = adj_local.shape[-1]
    row_tiles = adj_local.shape[0]
    width = hop_feats.shape[2]
    slots = shuffle.shape[1]
    share = slots // devices
    inner = w_first.shape[0]
    hop_two = hop_feats[2]
    sent = hop_two.at[boundary_rows[0]].get(mode="promise_in_bounds")
    own = jnp.concatenate([w_first, w_second.T], axis=0)
    halo = lax.all_to_all(sent, BOTH, split_axis=0, concat_axis=0, tiled=True)
    rep_at = lax.axis_index("rep")
    pieces = jnp.stack(
        [own]
        + [
            lax.ppermute(own, "rep", [(i, (i + s) % num_rep) for i in range(num_rep)])
            for s in range(1, num_rep)
        ]
    )
    packed = jnp.concatenate(
        [
            lax.dynamic_index_in_dim(pieces, (rep_at - i + num_rep) % num_rep, 0, keepdims=False)
            for i in range(num_rep)
        ],
        axis=1,
    )
    near_sum = tile_sum(
        adj_local, local_cols, hop_two.reshape(row_tiles, tile, width), None, jnp.float32
    )
    (order,) = take_ints([train_ids[0]], shuffle[0], tile)
    targets, marks = take_ints([labels, labelled], order, tile)
    marks = marks.astype(jnp.float32)
    next_hop = tile_sum(adj_halo, halo_cols, halo.reshape(-1, tile, width), near_sum, jnp.bfloat16)
    batch = pick_rows(order, hop_feats, next_hop)
    first_whole, second_t = packed[:inner], packed[inner:]
    hidden_units = first_whole.shape[1]
    classes = second_t.shape[0]

    pre = jnp.dot(batch, first_whole, preferred_element_type=jnp.float32)
    pre3 = pre.reshape(devices, share, hidden_units)
    part_mean = jnp.mean(pre3, axis=1)
    part_dev = pre3 - part_mean[:, None, :]
    part_m2 = jnp.mean(part_dev * part_dev, axis=1)
    part_count = jnp.sum(marks.reshape(devices, share), axis=1)
    lane = 128
    count_cols = jnp.broadcast_to(part_count[:, None], (devices, lane))
    stats = jnp.concatenate([part_mean, part_m2, count_cols], axis=1)
    got = lax.all_to_all(stats, BOTH, split_axis=0, concat_axis=0, tiled=True)
    means = got[:, :hidden_units]
    mean = jnp.mean(means, axis=0, keepdims=True)
    off = means - mean
    var = jnp.mean(got[:, hidden_units : 2 * hidden_units] + off * off, axis=0, keepdims=True)
    total = jnp.maximum(jnp.sum(got[:, 2 * hidden_units :], axis=0, keepdims=True), 1.0)
    mine = jnp.concatenate([mean, lax.rsqrt(var + 1e-05), 1.0 / total], axis=1)
    every = gather_by_exchange(mine, BOTH, devices)
    mu = every[:, None, :hidden_units]
    rstd = every[:, None, hidden_units : 2 * hidden_units]
    inv_count = every[:, 2 * hidden_units]

    normed3 = (pre3 - mu) * rstd
    normed = normed3.reshape(slots, hidden_units)
    hidden = jnp.maximum(normed, 0.0).astype(jnp.bfloat16)
    logits = lax.dot_general(
        second_t, hidden, (((1,), (1,)), ((), ())), preferred_element_type=jnp.float32
    )
    row_max = jnp.max(logits, axis=0, keepdims=True)
    expos = jnp.exp(logits - row_max)
    totals = jnp.sum(expos, axis=0, keepdims=True)
    onehot = (lax.broadcasted_iota(jnp.int32, logits.shape, 0) == targets[None, :]).astype(jnp.float32)
    cross = jnp.log(totals[0]) + row_max[0] - jnp.sum(onehot * logits, axis=0)
    scale = marks * jnp.broadcast_to(inv_count[:, None], (devices, share)).reshape(slots)
    dlogits = ((expos / totals - onehot) * scale[None, :]).astype(jnp.bfloat16)
    dlogits = lax.optimization_barrier(dlogits)
    grad_two_full = lax.dot_general(
        hidden, dlogits, (((0,), (1,)), ((), ())), preferred_element_type=jnp.float32
    )
    g_two = grad_two_full.astype(jnp.bfloat16).reshape(num_rep, -1, classes)

    dhidden = contract_rows(dlogits, second_t)
    masked3 = jnp.where(normed > 0, dhidden, 0.0).reshape(devices, share, hidden_units)
    part_grad = jnp.mean(masked3, axis=1)
    part_proj = jnp.mean(masked3 * normed3, axis=1)
    losses = jnp.sum((marks * cross).reshape(devices, share), axis=1) / jnp.maximum(part_count, 1.0)
    loss_cols = jnp.broadcast_to(losses[:, None], (devices, lane))
    sums = lax.all_to_all(
        jnp.concatenate([part_grad, part_proj, loss_cols], axis=1),
        BOTH, split_axis=0, concat_axis=0, tiled=True,
    )
    loss = sums[:, 2 * hidden_units].reshape(1, devices)
    back = gather_by_exchange(
        jnp.mean(sums[:, : 2 * hidden_units], axis=0, keepdims=True), BOTH, devices
    )
    back, g_two = lax.optimization_barrier((back, g_two))
    g_two = lax.all_to_all(g_two, "rep", split_axis=0, concat_axis=0, tiled=True)
    mean_grad = back[:, None, :hidden_units]
    mean_proj = back[:, None, hidden_units:]
    dpre = ((masked3 - mean_grad - normed3 * mean_proj) * rstd).astype(jnp.bfloat16)
    grad_one_full = contract_rows(batch, dpre.reshape(slots, hidden_units))
    g_one = grad_one_full.astype(jnp.bfloat16).reshape(num_dom, -1, hidden_units)
    g_two = jnp.sum(g_two.astype(jnp.float32), axis=0).astype(jnp.bfloat16)
    span = hidden_units // num_rep
    g_two = jnp.pad(g_two, ((0, 0), (0, span - classes)))
    g_two = g_two.reshape(num_dom, num_rep, -1, span)
    short = g_two.shape[2]
    g_two = jnp.concatenate([g_two[:, i] for i in range(num_rep)], axis=2)
    long = g_one.shape[1]
    both = lax.all_to_all(
        jnp.concatenate([g_one, g_two], axis=1), "dom", split_axis=0, concat_axis=0, tiled=True
    )
    both = jnp.sum(both.astype(jnp.float32), axis=0)
    blocks = jnp.stack([both[:long, i * span : (i + 1) * span] for i in range(num_rep)])
    grad_one = lax.dynamic_index_in_dim(blocks, rep_at, 0, keepdims=False)
    for s in range(1, num_rep):
        block = lax.dynamic_index_in_dim(blocks, (rep_at + s) % num_rep, 0, keepdims=False)
        grad_one = grad_one + lax.ppermute(
            block, "rep", [(i, (i + s) % num_rep) for i in range(num_rep)]
        )
    g_two = jnp.concatenate(
        [both[long:, i * span : i * span + classes] for i in range(num_rep)], axis=0
    )
    grad_two = gather_by_exchange(g_two[None], "dom", num_dom).reshape(-1, classes)
    return (next_hop, loss, grad_one, grad_two)


def solution(mesh):
    placed = (
        P(None, BOTH, None),
        P(BOTH, None, None, None),
        P(BOTH, None),
        P(BOTH, None, None, None),
        P(BOTH, None),
        P(BOTH, None),
        P(BOTH, None),
        P(BOTH, None),
        P(BOTH),
        P(BOTH),
        P(None, "rep"),
        P("rep", None),
    )
    return jax.shard_map(
        shards,
        mesh=mesh,
        in_specs=placed,
        out_specs=(P(BOTH, None), P(BOTH, None), P("dom", "rep"), P("rep", None)),
        check_vma=False,
    )
```
